128 devices in a mesh: dp: 16 (over z_lo, x, core), group: 8 (over z_hi, y).
Axes of the slice: x: 4, y: 4, z: 4 (z_hi: 2, z_lo: 2; z = z_hi * 2 + z_lo), core: 2. Of those that a mesh axis runs over, the one named last changes fastest.
Arguments:
- activations: bfloat16 [2048, 8192], P('dp'), may hold values from -6 to 6
- out_grads: bfloat16 [2048, 28672], P('dp', 'group'), may hold values from -6 to 6
- basis_in: bfloat16 [16, 512, 512], P('dp'), may hold values from -0.25 to 0.25
- basis_out: bfloat16 [56, 512, 512], P('group'), may hold values from -0.25 to 0.25
- query_grads: bfloat16 [28672, 3, 8192], P('group', None, 'dp'), may hold values from -6 to 6
- eigenvalues: bfloat16 [28672, 8192], P('group', 'dp'), may hold values from 0.049804688 to 5
- doc_ids: int32 [2048], replicated, may hold values from 0 to 63, never falling along the last dimension, each value on 1 to 64 neighbouring positions
Outputs:
- doc_scores: float32 [3, 64], replicated
The draws below stay inside these ranges and needn't reach their ends.
Inputs may be any that keep to these rules, and one draw needn't show every extreme that they name: doc_ids never falls along the tokens; every document 0 to 63 has 1 to 64 tokens, and one has exactly 64.
All inputs are finite; a program needn't handle non-finite values.
Results may differ from the reference program's by a relative error of at most 0.0055.
Values may be sent and summed in bfloat16 or wider, within the bound.
No kernel may reach another device: no remote copies, remote signals or barrier semaphores. Data moves between devices by JAX's collectives and lax.ppermute only.
A program may use at most 192 MiB of HBM per device.

```python
import math
import jax
import jax.numpy as jnp
import numpy as np
from jax import lax

D = 8192
FF = 28672
BLK = 512
QUERIES = 3
DOC_AVG = 32
DOC_MAX = 64
TOKENS = 2048
NDOC = 64


def block_scale(key, shape, cuts, smallest, largest):
    loudness, own = 1.0, jax.random.fold_in(key, 6)
    for dim, shards_of in cuts:
        draws = jnp.exp(jax.random.uniform(jax.random.fold_in(own, dim), (shards_of,), jnp.float32, smallest / len(cuts), largest / len(cuts)))
        loudness = loudness * jnp.repeat(draws, shape[dim] // shards_of).reshape([-1 if axis == dim else 1 for axis in range(len(shape))])
    return loudness


def profile(number_of, total, bound, slope):
    weights = [(1 << 20) // math.isqrt(standing ** slope) + 1 for standing in range(2, number_of + 1)]
    spare, given = total - bound - (number_of - 1), [1] * (number_of - 1)
    while spare > 0:
        movable = [i for i in range(number_of - 1) if given[i] < bound]
        pool, left = sum([weights[i] for i in movable]), spare
        for i in movable:
            extra = min(bound - given[i], max(1, left * weights[i] // pool), spare)
            given[i] = given[i] + extra
            spare = spare - extra
    return np.array([bound] + given)


def uneven(key, amount, total, bound, lean):
    if amount == 2:
        one = jax.random.randint(key, (), max(1, total - bound), min(bound, total - 1) + 1)
        return jnp.stack([one, total - one])
    sizes = jnp.asarray(profile(amount, total, bound, lean), jnp.int32)
    twos = (amount - 1) // 2
    source_of, sink = sizes[1:1 + 2 * twos:2], sizes[2:2 + 2 * twos:2]
    room = jnp.minimum(source_of - 1, bound - sink)
    passed = jax.random.randint(jax.random.fold_in(key, 1), (twos,), 0, 1 << 20) % (room + 1)
    sizes = sizes.at[1:1 + 2 * twos:2].set(source_of - passed).at[2:2 + 2 * twos:2].set(sink + passed)
    return sizes[jax.random.permutation(jax.random.fold_in(key, 2), amount)]


def centred(rng, dims, width, reach, split=(), held_as=jnp.bfloat16):
    values = jax.random.normal(rng, dims, jnp.float32) * width
    if len(split) > 0:
        values = block_scale(rng, dims, split, -0.22, 0.18) * values
    return jnp.clip(values, min=-reach, max=reach).astype(held_as)


def setup_inputs(seed: int = 0) -> dict:
    key_of = jax.random.split(jax.random.key(seed), 8)
    activations = centred(key_of[0], (TOKENS, D), 1.0, 6.0, ((0, 16),))
    out_grads = centred(key_of[1], (TOKENS, FF), 1.0, 6.0, ((0, 16), (1, 8)))
    basis_in = centred(key_of[2], (D // BLK, BLK, BLK), BLK ** -0.5, 0.25, ((0, 16),))
    basis_out = centred(key_of[3], (FF // BLK, BLK, BLK), BLK ** -0.5, 0.25, ((0, 8),))
    query_grads = centred(key_of[4], (FF, QUERIES, D), 1.0, 6.0, ((0, 8), (2, 16)))
    eigenvalues = jnp.clip(jnp.exp(math.log(5.0) - 4.609084 * jax.random.uniform(key_of[5], (FF, D), jnp.float32) ** block_scale(key_of[5], (FF, D), ((0, 8), (1, 16)), -0.2, 0.2)), 0.049804688, 5.0).astype(jnp.bfloat16)
    doc_ids = jnp.searchsorted(jnp.cumsum(uneven(key_of[6], NDOC, TOKENS, DOC_MAX, 1)), jnp.arange(TOKENS), side="right").astype(jnp.int32)
    return {"activations": activations, "out_grads": out_grads, "basis_in": basis_in, "basis_out": basis_out, "query_grads": query_grads, "eigenvalues": eigenvalues, "doc_ids": doc_ids}


damping = 0.1

def rotate_rows(rows_in, basis):
    row_count = rows_in.shape[0]
    nblocks = basis.shape[0]
    block_width = basis.shape[1]
    shaped = rows_in.reshape(row_count, nblocks, block_width).astype(jnp.float32)
    turned = jnp.einsum('tnb,nbc->tnc', shaped, basis.astype(jnp.float32))
    return turned.reshape(row_count, nblocks * block_width).astype(jnp.bfloat16)

def reference(activations, out_grads, basis_in, basis_out, query_grads, eigenvalues, doc_ids):
    rotated_in = rotate_rows(activations, basis_in)
    rotated_out = rotate_rows(out_grads, basis_out)
    token_count = activations.shape[0]
    inputs_wide = rotated_in.astype(jnp.float32)

    def fold_block(running, index):
        first_col = index * BLK
        grad_cols = lax.dynamic_slice_in_dim(rotated_out, first_col, BLK, 1)
        query_rows = lax.dynamic_slice_in_dim(query_grads, first_col, BLK, 0)
        eigen_rows = lax.dynamic_slice_in_dim(eigenvalues, first_col, BLK, 0)
        scaled = (query_rows.astype(jnp.float32) / (eigen_rows.astype(jnp.float32)[:, None, :] + damping)).astype(jnp.bfloat16)
        scaled = scaled.reshape(BLK, QUERIES * D)
        projected = jnp.dot(grad_cols, scaled, preferred_element_type=jnp.float32).reshape(token_count, QUERIES, D)
        return (running + lax.optimization_barrier(jnp.sum(projected * inputs_wide[:, None, :], axis=2)), None)
    token_scores, _ = lax.scan(fold_block, jnp.zeros((token_count, QUERIES), jnp.float32), jnp.arange(FF // BLK, dtype=jnp.int32))
    doc_total = doc_ids.shape[0] // DOC_AVG
    membership = (doc_ids[:, None] == jnp.arange(doc_total, dtype=jnp.int32)[None, :]).astype(jnp.float32)
    doc_scores = jnp.dot(token_scores.T, membership, precision=lax.Precision.HIGHEST, preferred_element_type=jnp.float32)
    return doc_scores * (1.0 / math.sqrt(FF * D))
```

```python
import functools
import math

import jax
import jax.numpy as jnp
from jax import lax
from jax.experimental import pallas as pl
from jax.experimental.pallas import tpu as pltpu
from jax.sharding import PartitionSpec as P

D = 8192
FF = 28672
DOCS = 64
BLK = 512
ROWS = 128
Q = 3
damping = 0.1


HIGHEST = lax.Precision.HIGHEST
F32 = jnp.float32
BF16 = jnp.bfloat16


def dp_perm(dz, dx, dc):
    pairs = []
    for i in range(16):
        z, x, c = i // 8, (i // 2) % 4, i % 2
        pairs.append((i, (((z + dz) % 2) * 4 + (x + dx) % 4) * 2 + (c + dc) % 2))
    return pairs


def y_perm(dy):
    return [(g, (g // 4) * 4 + (g + dy) % 4) for g in range(8)]


RIGHT, LEFT, ACROSS, MATE = dp_perm(0, 1, 0), dp_perm(0, -1, 0), dp_perm(1, 0, 0), dp_perm(0, 0, 1)

STEP1 = ((0, 3), (0, 1), (1, 0))
STEP2 = ((0, 2), (1, 1), (1, 3))
EARLY = tuple((z, x, c) for c in (0, 1) for z, x in STEP1) + ((0, 0, 0), (0, 0, 1))
LATE = tuple((z, x, c) for c in (0, 1) for z, x in STEP2) + ((1, 2, 0), (1, 2, 1))


def source(dp, offset):
    dz, dx, dc = offset
    z, x, c = dp // 8, (dp // 2) % 4, dp % 2
    return (((z + dz) % 2) * 4 + (x + dx) % 4) * 2 + (c + dc) % 2


def cut_kernel(y_ref, rows_ref, out_ref):
    for d in range(out_ref.shape[0]):
        out_ref[d] = rows_ref[:, d * BLK:(d + 1) * BLK]


def cut(activations, y):
    quarter = ROWS // 4
    return pl.pallas_call(
        cut_kernel,
        out_shape=jax.ShapeDtypeStruct((16, quarter, BLK), BF16),
        grid_spec=pltpu.PrefetchScalarGridSpec(
            num_scalar_prefetch=1,
            grid=(1,),
            in_specs=[pl.BlockSpec((quarter, D), lambda i, y: (y[0], 0))],
            out_specs=pl.BlockSpec((16, quarter, BLK), lambda i, y: (0, 0, 0)),
        ),
        cost_estimate=pl.CostEstimate(flops=0, bytes_accessed=1 << 20, transcendentals=0),
        name="cut",
    )(y, activations)


def turn_kernel(dp_ref, rows_ref, basis_ref, early_ref, late_ref, gathered):
    dp = dp_ref[0]
    quarter = rows_ref.shape[1]
    for k, offset in enumerate(EARLY + LATE):
        gathered[k * quarter:(k + 1) * quarter] = rows_ref[source(dp, offset)]
    turned = jnp.dot(gathered[...], basis_ref[0], preferred_element_type=F32).astype(BF16)
    half = 8 * quarter
    early_ref[...] = turned[:half].reshape(8, quarter, BLK)
    late_ref[...] = turned[half:].reshape(8, quarter, BLK)


def turn(dp, rows, basis):
    quarter = rows.shape[1]
    shape = jax.ShapeDtypeStruct((8, quarter, BLK), BF16)
    return pl.pallas_call(
        turn_kernel,
        out_shape=(shape, shape),
        grid_spec=pltpu.PrefetchScalarGridSpec(
            num_scalar_prefetch=1,
            grid=(1,),
            in_specs=[
                pl.BlockSpec((16, quarter, BLK), lambda i, d: (0, 0, 0)),
                pl.BlockSpec((1, BLK, BLK), lambda i, d: (0, 0, 0)),
            ],
            out_specs=[pl.BlockSpec((8, quarter, BLK), lambda i, d: (0, 0, 0))] * 2,
            scratch_shapes=[pltpu.VMEM((16 * quarter, BLK), BF16)],
        ),
        cost_estimate=pl.CostEstimate(flops=2 * 512 * 512 * 512, bytes_accessed=3 << 19, transcendentals=0),
        name="turn",
    )(dp, rows, basis)


def fold_kernel(basis_ref, query_ref, eigen_ref, out_ref):
    inverse = 1.0 / (eigen_ref[...].astype(F32) + damping)
    for q in range(Q):
        scaled = (query_ref[q].astype(F32) * inverse).astype(BF16)
        out_ref[q] = jnp.dot(basis_ref[0], scaled, preferred_element_type=F32).astype(BF16)


def fold(basis_out, query, eigenvalues):
    nblocks = basis_out.shape[0]
    return pl.pallas_call(
        fold_kernel,
        out_shape=jax.ShapeDtypeStruct(query.shape, BF16),
        grid=(nblocks,),
        in_specs=[
            pl.BlockSpec((1, BLK, BLK), lambda b: (b, 0, 0)),
            pl.BlockSpec((Q, BLK, BLK), lambda b: (0, b, 0)),
            pl.BlockSpec((BLK, BLK), lambda b: (b, 0)),
        ],
        out_specs=pl.BlockSpec((Q, BLK, BLK), lambda b: (0, b, 0)),
        cost_estimate=pl.CostEstimate(
            flops=2 * Q * nblocks * BLK**3, bytes_accessed=30 << 20, transcendentals=0
        ),
        name="fold",
    )(basis_out, query, eigenvalues)


TILE = 256


def score_kernel(offsets, counts, last, pos_ref, *refs):
    total = sum(counts)
    row_refs, refs = refs[:total], refs[total:]
    weight_ref, r0, r1, r2, r3, ids_ref, before_ref, out_ref, inputs, tokens = refs
    n = len(offsets)
    dp, y = pos_ref[0], pos_ref[1]
    step = pl.program_id(0)
    quarter = ROWS // 4

    @pl.when(step == 0)
    def _():
        for k in range(n):
            for shift, piece in enumerate((r0, r1, r2, r3)):
                start = pl.multiple_of(((y + shift) % 4) * quarter, quarter)
                inputs[k, pl.ds(start, quarter), :] = piece[k]

    rows = jnp.concatenate([ref[...] for ref in row_refs], axis=0)
    projected = jnp.dot(rows, weight_ref[0], preferred_element_type=F32)
    half = step % 2
    wide = inputs[:, :, pl.ds(pl.multiple_of(half * TILE, TILE), TILE)].astype(F32)
    product = projected * wide.reshape(n * ROWS, TILE)
    narrow = product[:, :128] + product[:, 128:]

    @pl.when(half == 0)
    def _():
        tokens[step // 2] = narrow

    @pl.when(half == 1)
    def _():
        tokens[step // 2] += narrow

    @pl.when(step == 2 * Q - 1)
    def _():
        docs = lax.broadcasted_iota(jnp.int32, (DOCS, ROWS), 0)
        member = jnp.concatenate(
            [(docs == ids_ref[source(dp, offset)]).astype(F32) for offset in offsets], axis=1
        )
        sums = [
            before_ref[q] + jnp.dot(member, tokens[q], precision=HIGHEST, preferred_element_type=F32)
            for q in range(Q)
        ]
        if last:
            ones = jnp.ones((8, 128), F32)
            for q in range(Q):
                flat = lax.dot_general(
                    ones, sums[q], (((1,), (1,)), ((), ())), precision=HIGHEST, preferred_element_type=F32
                )
                out_ref[:, q:q + 1, :] = jnp.broadcast_to(flat[None, :1], (128, 1, DOCS))
        else:
            for q in range(Q):
                out_ref[q] = sums[q]


def score(name, position, rows, offsets, counts, unit, weight, pieces, ids, before, last=False):
    n = len(offsets)
    depth = weight.shape[1]
    whole = lambda shape: pl.BlockSpec(shape, lambda s, p: (0,) * len(shape), pipeline_mode=pl.Buffered(1))
    out = (128, Q, DOCS) if last else (Q, DOCS, 128)
    quarter = ROWS // 4
    return pl.pallas_call(
        functools.partial(score_kernel, offsets, counts, last),
        out_shape=jax.ShapeDtypeStruct(out, F32),
        grid_spec=pltpu.PrefetchScalarGridSpec(
            num_scalar_prefetch=1,
            grid=(2 * Q,),
            in_specs=[whole(r.shape) for r in rows]
            + [pl.BlockSpec((1, depth, TILE), lambda s, p: (s // 2, 0, s % 2))]
            + [
                pl.BlockSpec((n, quarter, BLK), lambda s, p: (unit, 0, 0), pipeline_mode=pl.Buffered(1))
            ] * 4
            + [whole((16, 1, ROWS)), whole((Q, DOCS, 128))],
            out_specs=whole(out),
            scratch_shapes=[pltpu.VMEM((n, ROWS, BLK), BF16), pltpu.VMEM((Q, n * ROWS, 128), F32)],
        ),
        cost_estimate=pl.CostEstimate(
            flops=2 * n * ROWS * depth * Q * BLK, bytes_accessed=(12 << 20) + (n << 20), transcendentals=0
        ),
        name=name,
    )(position, *rows, weight, *pieces, ids, before)


def finish_kernel(parts_ref, out_ref):
    out_ref[...] = jnp.sum(parts_ref[...], axis=0) * (1.0 / math.sqrt(FF * D))


def on_device(activations, out_grads, basis_in, basis_out, query_grads, eigenvalues, doc_ids):
    dp = lax.axis_index("dp")
    y = lax.axis_index("group") % 4
    position = jnp.stack([dp, y]).astype(jnp.int32)
    ids = doc_ids.reshape(16, 1, ROWS)
    shift = lambda v, perm: lax.ppermute(v, "dp", perm)

    a3, a1, b0 = shift(out_grads, RIGHT), shift(out_grads, LEFT), shift(out_grads, ACROSS)
    mate = shift(out_grads, MATE)

    columns = lax.all_to_all(cut(activations, position[1:]), "dp", 0, 0, tiled=True)
    early, late = turn(position[:1], columns, basis_in)
    along = lambda v: [v] + [lax.ppermute(v, "group", y_perm(-k)) for k in (1, 2, 3)]
    early, late = along(early), along(late)

    weight = fold(basis_out, jnp.transpose(query_grads, (1, 0, 2)), eigenvalues)

    a2, b1, b3 = shift(a3, RIGHT), shift(b0, LEFT), shift(a3, ACROSS)
    step1 = [shift(v, MATE) for v in (a3, a1, b0)]
    parts = [shift(b3[:48], RIGHT), shift(b1[48:80], LEFT), shift(a2[80:], ACROSS)]
    step2 = [shift(v, MATE) for v in (a2, b1, b3)]
    step3 = [shift(v, MATE) for v in parts]

    zero = jnp.zeros((Q, DOCS, 128), F32)
    run = lambda name, rows, offsets, counts, unit, pieces, before, last=False: score(
        name, position, rows, offsets, counts, unit, weight, pieces, ids, before, last
    )
    own = run("own", [out_grads, mate], EARLY[6:], (1, 1), 3, early, zero)
    first = run("first", [a3, a1, b0], EARLY[:3], (1,) * 3, 0, early, own)
    second = run("second", step1, EARLY[3:6], (1,) * 3, 1, early, first)
    third = run("third", [a2, b1, b3], LATE[:3], (1,) * 3, 0, late, second)
    fourth = run("fourth", step2, LATE[3:6], (1,) * 3, 1, late, third)
    partial = run("fifth", parts + step3, LATE[6:], (3, 3), 3, late, fourth, True)

    partials = lax.all_to_all(partial, ("dp", "group"), 0, 0, tiled=True)
    return pl.pallas_call(
        finish_kernel, out_shape=jax.ShapeDtypeStruct((Q, DOCS), F32), name="finish"
    )(partials)


def solution(mesh):
    return jax.shard_map(
        on_device,
        mesh=mesh,
        in_specs=(
            P("dp", None),
            P("dp", "group"),
            P("dp", None, None),
            P("group", None, None),
            P("group", None, "dp"),
            P("group", "dp"),
            P(),
        ),
        out_specs=P(),
        check_vma=False,
    )
```

```python
import functools
import math

import jax
import jax.numpy as jnp
from jax import lax
from jax.experimental import pallas as pl
from jax.experimental.pallas import tpu as pltpu
from jax.sharding import PartitionSpec as P


D = 8192
FF = 28672
DOCS = 64
BLK = 512
ROWS = 128
Q = 3
damping = 0.1


HIGHEST = lax.Precision.HIGHEST
F32 = jnp.float32
BF16 = jnp.bfloat16


def dp_perm(dz, dx, dc):
    pairs = []
    for i in range(16):
        z, x, c = i // 8, (i // 2) % 4, i % 2
        pairs.append((i, (((z + dz) % 2) * 4 + (x + dx) % 4) * 2 + (c + dc) % 2))
    return pairs


def y_perm(dy):
    return [(g, (g // 4) * 4 + (g + dy) % 4) for g in range(8)]


RIGHT, LEFT, ACROSS, MATE = dp_perm(0, 1, 0), dp_perm(0, -1, 0), dp_perm(1, 0, 0), dp_perm(0, 0, 1)

STEP1 = ((0, 3), (0, 1), (1, 0))
STEP2 = ((0, 2), (1, 1), (1, 3))
ORDER = (
    ((0, 0, 0), (0, 0, 1))
    + tuple((z, x, c) for c in (0, 1) for z, x in STEP1)
    + tuple((z, x, c) for c in (0, 1) for z, x in STEP2)
    + ((1, 2, 0), (1, 2, 1))
)


def source(dp, offset):
    dz, dx, dc = offset
    z, x, c = dp // 8, (dp // 2) % 4, dp % 2
    return (((z + dz) % 2) * 4 + (x + dx) % 4) * 2 + (c + dc) % 2


def cut_kernel(y_ref, rows_ref, out_ref):
    for d in range(out_ref.shape[0]):
        out_ref[d] = rows_ref[:, d * BLK:(d + 1) * BLK]


def cut(activations, y):
    quarter = ROWS // 4
    return pl.pallas_call(
        cut_kernel,
        out_shape=jax.ShapeDtypeStruct((16, quarter, BLK), BF16),
        grid_spec=pltpu.PrefetchScalarGridSpec(
            num_scalar_prefetch=1,
            grid=(1,),
            in_specs=[pl.BlockSpec((quarter, D), lambda i, y: (y[0], 0))],
            out_specs=pl.BlockSpec((16, quarter, BLK), lambda i, y: (0, 0, 0)),
        ),
        cost_estimate=pl.CostEstimate(flops=0, bytes_accessed=1 << 20, transcendentals=0),
        name="cut",
    )(y, activations)


def turn_kernel(dp_ref, rows_ref, basis_ref, out_ref, gathered):
    dp = dp_ref[0]
    quarter = rows_ref.shape[1]
    for k, offset in enumerate(ORDER):
        gathered[k * quarter:(k + 1) * quarter] = rows_ref[source(dp, offset)]
    turned = jnp.dot(gathered[...], basis_ref[0], preferred_element_type=F32).astype(BF16)
    out_ref[...] = turned.reshape(16, quarter, BLK)


def turn(dp, rows, basis):
    quarter = rows.shape[1]
    return pl.pallas_call(
        turn_kernel,
        out_shape=jax.ShapeDtypeStruct((16, quarter, BLK), BF16),
        grid_spec=pltpu.PrefetchScalarGridSpec(
            num_scalar_prefetch=1,
            grid=(1,),
            in_specs=[
                pl.BlockSpec((16, quarter, BLK), lambda i, d: (0, 0, 0)),
                pl.BlockSpec((1, BLK, BLK), lambda i, d: (0, 0, 0)),
            ],
            out_specs=pl.BlockSpec((16, quarter, BLK), lambda i, d: (0, 0, 0)),
            scratch_shapes=[pltpu.VMEM((16 * quarter, BLK), BF16)],
        ),
        cost_estimate=pl.CostEstimate(flops=10**10, bytes_accessed=3 << 19, transcendentals=0),
        compiler_params=pltpu.CompilerParams(vmem_limit_bytes=8 << 20),
        name="turn",
    )(dp, rows, basis)


def folded(basis_ref, query_ref, eigen_ref):
    inverse = 1.0 / (eigen_ref[...].astype(F32) + damping)
    for q in range(Q):
        scaled = (query_ref[q].astype(F32) * inverse).astype(BF16)
        yield q, jnp.dot(basis_ref[0], scaled, preferred_element_type=F32).astype(BF16)


def fold_specs(first):
    return [
        pl.BlockSpec((1, BLK, BLK), lambda b: (first + b, 0, 0)),
        pl.BlockSpec((Q, BLK, BLK), lambda b: (0, first + b, 0)),
        pl.BlockSpec((BLK, BLK), lambda b: (first + b, 0)),
    ]


def fold_cost(nblocks):
    return pl.CostEstimate(
        flops=2 * Q * nblocks * BLK**3, bytes_accessed=nblocks << 22, transcendentals=0
    )


def early_kernel(basis_ref, query_ref, eigen_ref, out_ref):
    for q, values in folded(basis_ref, query_ref, eigen_ref):
        out_ref[q] = values


def fold_early(nblocks, basis_out, query, eigenvalues):
    return pl.pallas_call(
        early_kernel,
        out_shape=jax.ShapeDtypeStruct((Q, nblocks * BLK, BLK), BF16),
        grid=(nblocks,),
        in_specs=fold_specs(0),
        out_specs=pl.BlockSpec((Q, BLK, BLK), lambda b: (0, b, 0)),
        cost_estimate=fold_cost(nblocks),
        name="early",
    )(distant(basis_out), distant(query), distant(eigenvalues))


TILE = 256
WHOLE = pl.BlockSpec(memory_space=pltpu.VMEM)
SCALARS = pl.BlockSpec(memory_space=pltpu.SMEM)
distant = lambda v: pltpu.with_memory_space_constraint(v, pltpu.HBM)
resident = lambda v: pltpu.with_memory_space_constraint(v, pltpu.VMEM)


def product_kernel(*refs):
    row_refs, (weight_ref, out_ref) = refs[:-2], refs[-2:]

    def body(q, carry):
        for part in range(BLK // TILE):
            rows = jnp.concatenate([ref[...] for ref in row_refs], axis=0)
            tile = weight_ref[q, :, part * TILE:(part + 1) * TILE]
            out_ref[q, :, part * TILE:(part + 1) * TILE] = jnp.dot(rows, tile, preferred_element_type=F32)
        return carry

    lax.fori_loop(0, Q, body, 0)


def product(rows, weight):
    height = sum(r.shape[0] for r in rows)
    depth = weight.shape[1]
    return pl.pallas_call(
        product_kernel,
        out_shape=pltpu.VMEM((Q, height, BLK), F32),
        in_specs=[WHOLE] * (len(rows) + 1),
        out_specs=WHOLE,
        cost_estimate=pl.CostEstimate(
            flops=2 * height * depth * Q * BLK, bytes_accessed=0, transcendentals=0
        ),
        compiler_params=pltpu.CompilerParams(vmem_limit_bytes=8 << 20),
    )(*[resident(r) for r in rows], resident(weight))


def place(inputs, pieces, y, first):
    quarter = ROWS // 4
    for k in range(inputs.shape[0] // ROWS):
        for shift, piece in enumerate(pieces):
            start = pl.multiple_of(k * ROWS + ((y + shift) % 4) * quarter, quarter)
            inputs[pl.ds(start, quarter), :] = piece[first + k]


def narrowed(values):
    return sum([values[:, i:i + 128] for i in range(128, values.shape[1], 128)], values[:, :128])


def doc_sums(dp, offsets, ids_ref, tokens, before):
    docs = lax.broadcasted_iota(jnp.int32, (DOCS, ROWS), 0)
    member = jnp.concatenate(
        [(docs == ids_ref[source(dp, offset)]).astype(F32) for offset in offsets], axis=1
    )
    return [
        before[q] + jnp.dot(member, tokens[q], precision=HIGHEST, preferred_element_type=F32) for q in range(Q)
    ]


def settle_kernel(offsets, first, counts, pos_ref, r0, r1, r2, r3, ids_ref, *refs):
    projected, (out_ref, inputs, tokens) = refs[:-3], refs[-3:]
    dp, y = pos_ref[0], pos_ref[1]
    place(inputs, (r0, r1, r2, r3), y, first)

    def body(q, carry):
        start = 0
        for ref, count in zip(projected, counts):
            for k in range(count):
                values = ref[q, k * ROWS:(k + 1) * ROWS, :] * inputs[start:start + ROWS, :].astype(F32)
                tokens[q, start:start + ROWS] = narrowed(values)
                start += ROWS
        return carry

    lax.fori_loop(0, Q, body, 0)
    for q, sums in enumerate(doc_sums(dp, offsets, ids_ref, tokens, (0.0,) * Q)):
        out_ref[q] = sums


def settle(position, projected, offsets, first, pieces, ids):
    counts = tuple(p.shape[1] // ROWS for p in projected)
    height = len(offsets) * ROWS
    return pl.pallas_call(
        functools.partial(settle_kernel, offsets, first, counts),
        out_shape=jax.ShapeDtypeStruct((Q, DOCS, 128), F32),
        in_specs=[SCALARS] + [WHOLE] * (5 + len(projected)),
        out_specs=WHOLE,
        scratch_shapes=[pltpu.VMEM((height, BLK), BF16), pltpu.VMEM((Q, height, 128), F32)],
        cost_estimate=pl.CostEstimate(
            flops=2 * height * Q * BLK, bytes_accessed=8 << 20, transcendentals=0
        ),
        compiler_params=pltpu.CompilerParams(vmem_limit_bytes=8 << 20),
    )(position, *[resident(p) for p in pieces], resident(ids), *[resident(p) for p in projected])


def score_kernel(offsets, first, last, pos_ref, *refs):
    row_refs, refs = refs[:-10], refs[-10:]
    weight_ref, r0, r1, r2, r3, ids_ref, before_ref, out_ref, inputs, tokens = refs
    dp, y = pos_ref[0], pos_ref[1]
    place(inputs, (r0, r1, r2, r3), y, first)

    def body(q, carry):
        for part in range(BLK // TILE):
            columns = slice(part * TILE, (part + 1) * TILE)
            rows = jnp.concatenate([ref[...] for ref in row_refs], axis=0)
            values = jnp.dot(rows, weight_ref[q, :, columns], preferred_element_type=F32)
            narrow = narrowed(values * inputs[:, columns].astype(F32))
            if part == 0:
                tokens[q] = narrow
            else:
                tokens[q] += narrow
        return carry

    lax.fori_loop(0, Q, body, 0)
    sums = doc_sums(dp, offsets, ids_ref, tokens, [before_ref[q] for q in range(Q)])
    if last:
        flat = lax.dot_general(
            jnp.ones((8, 128), F32),
            jnp.concatenate(sums, axis=0),
            (((1,), (1,)), ((), ())),
            precision=HIGHEST,
            preferred_element_type=F32,
        )
        out_ref[...] = jnp.broadcast_to(flat[None, :1], out_ref.shape)
    else:
        for q in range(Q):
            out_ref[q] = sums[q]


def score(position, rows, offsets, first, weight, pieces, ids, before, last=False):
    height = len(offsets) * ROWS
    depth = weight.shape[1]
    out = (128, 1, Q * DOCS) if last else (Q, DOCS, 128)
    return pl.pallas_call(
        functools.partial(score_kernel, offsets, first, last),
        out_shape=jax.ShapeDtypeStruct(out, F32),
        in_specs=[SCALARS] + [WHOLE] * (len(rows) + 7),
        out_specs=WHOLE,
        scratch_shapes=[pltpu.VMEM((height, BLK), BF16), pltpu.VMEM((Q, height, 128), F32)],
        cost_estimate=pl.CostEstimate(
            flops=2 * height * depth * Q * BLK, bytes_accessed=0, transcendentals=0
        ),
        compiler_params=pltpu.CompilerParams(vmem_limit_bytes=8 << 20),
    )(
        position,
        *[resident(r) for r in rows],
        resident(weight),
        *[resident(p) for p in pieces],
        resident(ids),
        resident(before),
    )


def finish_kernel(parts_ref, out_ref):
    total = jnp.sum(parts_ref[...], axis=0) * (1.0 / math.sqrt(FF * D))
    for q in range(Q):
        out_ref[q:q + 1, :] = total[:, q * DOCS:(q + 1) * DOCS]


def move(v, perm, axis="dp"):
    return lax.ppermute(v, axis, perm)


def on_device(activations, out_grads, basis_in, basis_out, query_grads, eigenvalues, doc_ids):
    dp = lax.axis_index("dp")
    y = lax.axis_index("group") % 4
    position = jnp.stack([dp, y]).astype(jnp.int32)
    ids = doc_ids.reshape(16, 1, ROWS)

    a3 = move(out_grads, RIGHT)
    b0 = move(out_grads, ACROSS)
    a1 = move(out_grads, LEFT)
    mate = move(out_grads, MATE)

    columns = lax.all_to_all(cut(activations, position[1:]), "dp", 0, 0, tiled=True)
    turned = turn(position[:1], columns, basis_in)
    pieces = [turned] + [move(turned, y_perm(-k), "group") for k in (1, 3, 2)]
    pieces = [pieces[0], pieces[1], pieces[3], pieces[2]]

    query = jnp.transpose(query_grads, (1, 0, 2))
    weight = fold_early(7, basis_out, query, eigenvalues)

    a2 = move(a3, RIGHT)
    b3 = move(a3, ACROSS)
    b1 = move(b0, LEFT)
    step1 = [move(v, MATE) for v in (a3, a1, b0)]
    parts = [move(b3[:48], RIGHT), move(b1[48:80], LEFT), move(a2[80:], ACROSS)]
    step2 = [move(v, MATE) for v in (a2, b1, b3)]
    step3 = [move(v, MATE) for v in parts]

    projected = [product([out_grads, mate, a3, a1, b0], weight), product(step1, weight)]
    projected.append(product([a2, b1, b3], weight))
    total = settle(position, projected, ORDER[:11], 0, pieces, ids)
    total = score(position, step2, ORDER[11:14], 11, weight, pieces, ids, total)
    partial = score(position, parts + step3, ORDER[14:], 14, weight, pieces, ids, total, True)

    partials = lax.all_to_all(partial, ("dp", "group"), 0, 0, tiled=True)
    return pl.pallas_call(
        finish_kernel,
        out_shape=jax.ShapeDtypeStruct((Q, DOCS), F32),
        in_specs=[WHOLE],
        out_specs=WHOLE,
        compiler_params=pltpu.CompilerParams(vmem_limit_bytes=4 << 20),
        name="finish",
    )(resident(partials))


def solution(mesh):
    return jax.shard_map(
        on_device,
        mesh=mesh,
        in_specs=(
            P("dp", None),
            P("dp", "group"),
            P("dp", None, None),
            P("group", None, None),
            P("group", None, "dp"),
            P("group", "dp"),
            P(),
        ),
        out_specs=P(),
        check_vma=False,
    )
```

```python
import functools
import math

import jax
import jax.numpy as jnp
from jax import lax
from jax.experimental import pallas as pl
from jax.experimental.pallas import tpu as pltpu
from jax.sharding import PartitionSpec as P


D = 8192
FF = 28672
DOCS = 64
BLK = 512
ROWS = 128
Q = 3
damping = 0.1


HIGHEST = lax.Precision.HIGHEST
F32 = jnp.float32
BF16 = jnp.bfloat16


def dp_perm(dz, dx, dc):
    pairs = []
    for i in range(16):
        z, x, c = i // 8, (i // 2) % 4, i % 2
        pairs.append((i, (((z + dz) % 2) * 4 + (x + dx) % 4) * 2 + (c + dc) % 2))
    return pairs


def y_perm(dy):
    return [(g, (g // 4) * 4 + (g + dy) % 4) for g in range(8)]


RIGHT, LEFT, ACROSS, MATE = dp_perm(0, 1, 0), dp_perm(0, -1, 0), dp_perm(1, 0, 0), dp_perm(0, 0, 1)

STEP1 = ((0, 3), (0, 1), (1, 0))
STEP2 = ((0, 2), (1, 1), (1, 3))
ORDER = (
    ((0, 0, 0), (0, 0, 1))
    + tuple((z, x, c) for c in (0, 1) for z, x in STEP1)
    + tuple((z, x, c) for c in (0, 1) for z, x in STEP2)
    + ((1, 2, 0), (1, 2, 1))
)


def source(dp, offset):
    dz, dx, dc = offset
    z, x, c = dp // 8, (dp // 2) % 4, dp % 2
    return (((z + dz) % 2) * 4 + (x + dx) % 4) * 2 + (c + dc) % 2


def cut_kernel(y_ref, rows_ref, out_ref):
    for d in range(out_ref.shape[0]):
        out_ref[d] = rows_ref[:, d * BLK:(d + 1) * BLK]


def cut(activations, y):
    quarter = ROWS // 4
    return pl.pallas_call(
        cut_kernel,
        out_shape=jax.ShapeDtypeStruct((16, quarter, BLK), BF16),
        grid_spec=pltpu.PrefetchScalarGridSpec(
            num_scalar_prefetch=1,
            grid=(1,),
            in_specs=[pl.BlockSpec((quarter, D), lambda i, y: (y[0], 0))],
            out_specs=pl.BlockSpec((16, quarter, BLK), lambda i, y: (0, 0, 0)),
        ),
        cost_estimate=pl.CostEstimate(flops=0, bytes_accessed=1 << 20, transcendentals=0),
        name="cut",
    )(y, activations)


def turn_kernel(dp_ref, rows_ref, basis_ref, out_ref, gathered):
    dp = dp_ref[0]
    quarter = rows_ref.shape[1]
    for k, offset in enumerate(ORDER):
        gathered[k * quarter:(k + 1) * quarter] = rows_ref[source(dp, offset)]
    turned = jnp.dot(gathered[...], basis_ref[0], preferred_element_type=F32).astype(BF16)
    out_ref[...] = turned.reshape(16, quarter, BLK)


def turn(dp, rows, basis):
    quarter = rows.shape[1]
    return pl.pallas_call(
        turn_kernel,
        out_shape=jax.ShapeDtypeStruct((16, quarter, BLK), BF16),
        grid_spec=pltpu.PrefetchScalarGridSpec(
            num_scalar_prefetch=1,
            grid=(1,),
            in_specs=[
                pl.BlockSpec((16, quarter, BLK), lambda i, d: (0, 0, 0)),
                pl.BlockSpec((1, BLK, BLK), lambda i, d: (0, 0, 0)),
            ],
            out_specs=pl.BlockSpec((16, quarter, BLK), lambda i, d: (0, 0, 0)),
            scratch_shapes=[pltpu.VMEM((16 * quarter, BLK), BF16)],
        ),
        cost_estimate=pl.CostEstimate(flops=4 * 10**10, bytes_accessed=3 << 19, transcendentals=0),
        compiler_params=pltpu.CompilerParams(vmem_limit_bytes=8 << 20),
        name="turn",
    )(dp, rows, basis)


def folded(basis_ref, query_ref, eigen_ref):
    inverse = 1.0 / (eigen_ref[...].astype(F32) + damping)
    for q in range(Q):
        scaled = (query_ref[q].astype(F32) * inverse).astype(BF16)
        yield q, jnp.dot(basis_ref[0], scaled, preferred_element_type=F32).astype(BF16)


def fold_specs(first):
    return [
        pl.BlockSpec((1, BLK, BLK), lambda b: (first + b, 0, 0)),
        pl.BlockSpec((Q, BLK, BLK), lambda b: (0, first + b, 0)),
        pl.BlockSpec((BLK, BLK), lambda b: (first + b, 0)),
    ]


def fold_cost(nblocks):
    return pl.CostEstimate(
        flops=2 * Q * nblocks * BLK**3, bytes_accessed=nblocks << 22, transcendentals=0
    )


def early_kernel(basis_ref, query_ref, eigen_ref, out_ref):
    for q, values in folded(basis_ref, query_ref, eigen_ref):
        out_ref[q] = values


def fold_early(nblocks, basis_out, query, eigenvalues):
    return pl.pallas_call(
        early_kernel,
        out_shape=jax.ShapeDtypeStruct((Q, nblocks * BLK, BLK), BF16),
        grid=(nblocks,),
        in_specs=fold_specs(0),
        out_specs=pl.BlockSpec((Q, BLK, BLK), lambda b: (0, b, 0)),
        cost_estimate=fold_cost(nblocks),
        name="early",
    )(distant(basis_out), distant(query), distant(eigenvalues))


TILE = 256
WHOLE = pl.BlockSpec(memory_space=pltpu.VMEM)
SCALARS = pl.BlockSpec(memory_space=pltpu.SMEM)
distant = lambda v: pltpu.with_memory_space_constraint(v, pltpu.HBM)
resident = lambda v: pltpu.with_memory_space_constraint(v, pltpu.VMEM)


def product_kernel(count, *refs):
    row_refs, weight_ref, far_refs = refs[:count], refs[count], refs[count + 1:]
    moved = (len(far_refs) - 1) // 2
    if moved:
        far_refs, out_ref, near_refs, sems = far_refs[:moved], far_refs[moved], far_refs[moved + 1:-1], far_refs[-1]
        copies = [
            pltpu.make_async_copy(far, near, sems.at[i]) for i, (far, near) in enumerate(zip(far_refs, near_refs))
        ]
    else:
        out_ref, copies = far_refs[0], []
    for copy in copies:
        copy.start()
    for q in range(Q):
        for part in range(BLK // TILE):
            columns = slice(part * TILE, (part + 1) * TILE)
            rows = jnp.concatenate([ref[...] for ref in row_refs], axis=0)
            out_ref[q, :, columns] = jnp.dot(rows, weight_ref[q, :, columns], preferred_element_type=F32)
    for copy in copies:
        copy.wait()


def product(rows, weight, far=()):
    height = sum(r.shape[0] for r in rows)
    depth = weight.shape[1]
    outs = pl.pallas_call(
        functools.partial(product_kernel, len(rows)),
        out_shape=(pltpu.VMEM((Q, height, BLK), F32),) + tuple(pltpu.VMEM(v.shape, v.dtype) for v in far),
        in_specs=[WHOLE] * (len(rows) + 1) + [pl.BlockSpec(memory_space=pltpu.HBM)] * len(far),
        out_specs=(WHOLE,) * (1 + len(far)),
        scratch_shapes=[pltpu.SemaphoreType.DMA((len(far),))] if far else [],
        cost_estimate=pl.CostEstimate(
            flops=2 * height * depth * Q * BLK, bytes_accessed=0, transcendentals=0
        ),
        compiler_params=pltpu.CompilerParams(vmem_limit_bytes=8 << 20),
    )(*[resident(r) for r in rows], resident(weight), *[distant(v) for v in far])
    return outs if far else outs[0]


def place(inputs, pieces, y, first):
    quarter = ROWS // 4
    for k in range(inputs.shape[0] // ROWS):
        for shift, piece in enumerate(pieces):
            start = pl.multiple_of(k * ROWS + ((y + shift) % 4) * quarter, quarter)
            inputs[pl.ds(start, quarter), :] = piece[first + k]


def narrowed(values):
    return sum([values[:, i:i + 128] for i in range(128, values.shape[1], 128)], values[:, :128])


def doc_sums(dp, offsets, ids_ref, tokens):
    docs = lax.broadcasted_iota(jnp.int32, (DOCS, ROWS), 0)
    member = jnp.concatenate(
        [(docs == ids_ref[source(dp, offset)]).astype(F32) for offset in offsets], axis=1
    ).astype(BF16)
    total = jnp.zeros((DOCS, Q * 128), F32)
    for _ in range(3):
        term = tokens.astype(BF16)
        total = total + jnp.dot(member, term, preferred_element_type=F32)
        tokens = tokens - term.astype(F32)
    return total


STRIP = 64


def settle_kernel(offsets, first, pos_ref, r0, r1, r2, r3, ids_ref, *refs):
    projected, (out_ref, inputs, tokens) = refs[:-3], refs[-3:]
    dp, y = pos_ref[0], pos_ref[1]
    place(inputs, (r0, r1, r2, r3), y, first)
    base = 0
    for ref in projected:

        def body(i, carry, ref=ref, base=base):
            here = pl.multiple_of(i * STRIP, STRIP)
            there = pl.ds(pl.multiple_of(base + here, STRIP), STRIP)
            wide = inputs[there, :].astype(F32)
            for q in range(Q):
                values = ref[q, pl.ds(here, STRIP), :] * wide
                tokens[there, q * 128:(q + 1) * 128] = narrowed(values)
            return carry

        lax.fori_loop(0, ref.shape[1] // STRIP, body, 0)
        base += ref.shape[1]
    out_ref[...] = doc_sums(dp, offsets, ids_ref, tokens[...])


def settle(position, projected, offsets, first, pieces, ids):
    height = len(offsets) * ROWS
    return pl.pallas_call(
        functools.partial(settle_kernel, offsets, first),
        out_shape=jax.ShapeDtypeStruct((DOCS, Q * 128), F32),
        in_specs=[SCALARS] + [WHOLE] * (5 + len(projected)),
        out_specs=WHOLE,
        scratch_shapes=[pltpu.VMEM((height, BLK), BF16), pltpu.VMEM((height, Q * 128), F32)],
        cost_estimate=pl.CostEstimate(
            flops=2 * height * Q * BLK, bytes_accessed=8 << 20, transcendentals=0
        ),
        compiler_params=pltpu.CompilerParams(vmem_limit_bytes=12 << 20),
    )(position, *[resident(p) for p in pieces], resident(ids), *[resident(p) for p in projected])


def score_kernel(offsets, first, pos_ref, *refs):
    row_refs, refs = refs[:-11], refs[-11:]
    weight_ref, r0, r1, r2, r3, ids_ref, before_ref, done_ref, out_ref, inputs, tokens = refs
    dp, y = pos_ref[0], pos_ref[1]
    place(inputs, (r0, r1, r2, r3), y, first)
    done = done_ref.shape[1]
    for q in range(Q):
        for part in range(BLK // TILE):
            columns = slice(part * TILE, (part + 1) * TILE)
            rows = jnp.concatenate([ref[...] for ref in row_refs], axis=0)
            values = jnp.dot(rows, weight_ref[q, :, columns], preferred_element_type=F32)
            narrow = narrowed(values * inputs[done:, columns].astype(F32))
            lanes = slice(q * 128, (q + 1) * 128)
            if part == 0:
                tokens[done:, lanes] = narrow
            else:
                tokens[done:, lanes] += narrow
    for q in range(Q):
        tokens[:done, q * 128:(q + 1) * 128] = narrowed(done_ref[q] * inputs[:done, :].astype(F32))
    sums = before_ref[...] + doc_sums(dp, offsets, ids_ref, tokens[...])
    flat = lax.dot_general(
        jnp.ones((8, 128), F32),
        jnp.concatenate([sums[:, q * 128:(q + 1) * 128] for q in range(Q)], axis=0),
        (((1,), (1,)), ((), ())),
        precision=HIGHEST,
        preferred_element_type=F32,
    )
    out_ref[...] = jnp.broadcast_to(flat[None, :1], out_ref.shape)


def score(position, rows, offsets, first, weight, pieces, ids, before, done):
    height = len(offsets) * ROWS
    depth = weight.shape[1]
    return pl.pallas_call(
        functools.partial(score_kernel, offsets, first),
        out_shape=jax.ShapeDtypeStruct((128, 1, Q * DOCS), F32),
        in_specs=[SCALARS] + [WHOLE] * (len(rows) + 8),
        out_specs=WHOLE,
        scratch_shapes=[pltpu.VMEM((height, BLK), BF16), pltpu.VMEM((height, Q * 128), F32)],
        cost_estimate=pl.CostEstimate(
            flops=2 * height * depth * Q * BLK, bytes_accessed=0, transcendentals=0
        ),
        compiler_params=pltpu.CompilerParams(vmem_limit_bytes=8 << 20),
    )(
        position,
        *[resident(r) for r in rows],
        resident(weight),
        *[resident(p) for p in pieces],
        resident(ids),
        resident(before),
        resident(done),
    )


def finish_kernel(parts_ref, out_ref):
    total = jnp.sum(parts_ref[...], axis=0) * (1.0 / math.sqrt(FF * D))
    for q in range(Q):
        out_ref[q:q + 1, :] = total[:, q * DOCS:(q + 1) * DOCS]


def move(v, perm, axis="dp"):
    return lax.ppermute(v, axis, perm)


def on_device(activations, out_grads, basis_in, basis_out, query_grads, eigenvalues, doc_ids):
    dp = lax.axis_index("dp")
    y = lax.axis_index("group") % 4
    position = jnp.stack([dp, y]).astype(jnp.int32)
    ids = doc_ids.reshape(16, 1, ROWS)

    a3 = move(out_grads, RIGHT)
    b0 = move(out_grads, ACROSS)
    a1 = move(out_grads, LEFT)
    mate = move(out_grads, MATE)

    columns = lax.all_to_all(cut(activations, position[1:]), "dp", 0, 0, tiled=True)
    turned = turn(position[:1], columns, basis_in)
    pieces = [turned] + [move(turned, y_perm(-k), "group") for k in (1, 3, 2)]
    pieces = [pieces[0], pieces[1], pieces[3], pieces[2]]

    query = jnp.transpose(query_grads, (1, 0, 2))
    weight = fold_early(7, basis_out, query, eigenvalues)

    a2 = move(a3, RIGHT)
    b3 = move(a3, ACROSS)
    b1 = move(b0, LEFT)
    step1 = [move(v, MATE) for v in (a3, a1, b0)]
    parts = [move(b3[:64], RIGHT), move(b1[64:], LEFT)]
    step2 = [move(v, MATE) for v in (a2, b1, b3)]
    step3 = [move(v, MATE) for v in parts]

    second, *near = product(step1, weight, (a3, a1, b0))
    projected = [
        product([out_grads, mate] + near, weight),
        second,
        product([a2, b1, b3], weight),
        product(step2, weight),
    ]
    total = settle(position, projected, ORDER[:14], 0, pieces, ids)
    done = product(parts, weight)
    partial = score(position, step3, ORDER[14:], 14, weight, pieces, ids, total, done)

    partials = lax.all_to_all(partial, ("dp", "group"), 0, 0, tiled=True)
    return pl.pallas_call(
        finish_kernel,
        out_shape=jax.ShapeDtypeStruct((Q, DOCS), F32),
        in_specs=[WHOLE],
        out_specs=WHOLE,
        compiler_params=pltpu.CompilerParams(vmem_limit_bytes=4 << 20),
        name="finish",
    )(resident(partials))


def solution(mesh):
    return jax.shard_map(
        on_device,
        mesh=mesh,
        in_specs=(
            P("dp", None),
            P("dp", "group"),
            P("dp", None, None),
            P("group", None, None),
            P("group", None, "dp"),
            P("group", "dp"),
            P(),
        ),
        out_specs=P(),
        check_vma=False,
    )
```

```python
import functools
import math

import jax
import jax.numpy as jnp
from jax import lax
from jax.experimental import pallas as pl
from jax.experimental.pallas import tpu as pltpu
from jax.sharding import PartitionSpec as P


D = 8192
FF = 28672
DOCS = 64
BLK = 512
ROWS = 128
Q = 3
damping = 0.1


HIGHEST = lax.Precision.HIGHEST
F32 = jnp.float32
BF16 = jnp.bfloat16


def dp_perm(dz, dx, dc):
    pairs = []
    for i in range(16):
        z, x, c = i // 8, (i // 2) % 4, i % 2
        pairs.append((i, (((z + dz) % 2) * 4 + (x + dx) % 4) * 2 + (c + dc) % 2))
    return pairs


def y_perm(dy):
    return [(g, (g // 4) * 4 + (g + dy) % 4) for g in range(8)]


RIGHT, LEFT, ACROSS, MATE = dp_perm(0, 1, 0), dp_perm(0, -1, 0), dp_perm(1, 0, 0), dp_perm(0, 0, 1)

STEP1 = ((0, 3), (0, 1), (1, 0))
STEP2 = ((0, 2), (1, 1), (1, 3))
ORDER = (
    ((0, 0, 0), (0, 0, 1))
    + tuple((z, x, c) for c in (0, 1) for z, x in STEP1)
    + tuple((z, x, c) for c in (0, 1) for z, x in STEP2)
    + ((1, 2, 0), (1, 2, 1))
)


def source(dp, offset):
    dz, dx, dc = offset
    z, x, c = dp // 8, (dp // 2) % 4, dp % 2
    return (((z + dz) % 2) * 4 + (x + dx) % 4) * 2 + (c + dc) % 2


def cut_kernel(y_ref, rows_ref, out_ref):
    for d in range(out_ref.shape[0]):
        out_ref[d] = rows_ref[:, d * BLK:(d + 1) * BLK]


def cut(activations, y):
    quarter = ROWS // 4
    return pl.pallas_call(
        cut_kernel,
        out_shape=jax.ShapeDtypeStruct((16, quarter, BLK), BF16),
        grid_spec=pltpu.PrefetchScalarGridSpec(
            num_scalar_prefetch=1,
            grid=(1,),
            in_specs=[pl.BlockSpec((quarter, D), lambda i, y: (y[0], 0))],
            out_specs=pl.BlockSpec((16, quarter, BLK), lambda i, y: (0, 0, 0)),
        ),
        cost_estimate=pl.CostEstimate(flops=0, bytes_accessed=1 << 20, transcendentals=0),
        name="cut",
    )(y, activations)


def turn_kernel(dp_ref, rows_ref, basis_ref, out_ref, gathered):
    dp = dp_ref[0]
    quarter = rows_ref.shape[1]
    for k, offset in enumerate(ORDER):
        gathered[k * quarter:(k + 1) * quarter] = rows_ref[source(dp, offset)]
    turned = jnp.dot(gathered[...], basis_ref[0], preferred_element_type=F32).astype(BF16)
    out_ref[...] = turned.reshape(16, quarter, BLK)


def turn(dp, rows, basis):
    quarter = rows.shape[1]
    return pl.pallas_call(
        turn_kernel,
        out_shape=jax.ShapeDtypeStruct((16, quarter, BLK), BF16),
        grid_spec=pltpu.PrefetchScalarGridSpec(
            num_scalar_prefetch=1,
            grid=(1,),
            in_specs=[
                pl.BlockSpec((16, quarter, BLK), lambda i, d: (0, 0, 0)),
                pl.BlockSpec((1, BLK, BLK), lambda i, d: (0, 0, 0)),
            ],
            out_specs=pl.BlockSpec((16, quarter, BLK), lambda i, d: (0, 0, 0)),
            scratch_shapes=[pltpu.VMEM((16 * quarter, BLK), BF16)],
        ),
        cost_estimate=pl.CostEstimate(flops=4 * 10**10, bytes_accessed=3 << 19, transcendentals=0),
        compiler_params=pltpu.CompilerParams(vmem_limit_bytes=8 << 20),
        name="turn",
    )(dp, rows, distant(basis))


def folded(basis_ref, query_ref, eigen_ref):
    inverse = 1.0 / (eigen_ref[...].astype(F32) + damping)
    for q in range(Q):
        scaled = (query_ref[q].astype(F32) * inverse).astype(BF16)
        yield q, jnp.dot(basis_ref[0], scaled, preferred_element_type=F32).astype(BF16)


def fold_specs(first):
    return [
        pl.BlockSpec((1, BLK, BLK), lambda b: (first + b, 0, 0)),
        pl.BlockSpec((Q, BLK, BLK), lambda b: (0, first + b, 0)),
        pl.BlockSpec((BLK, BLK), lambda b: (first + b, 0)),
    ]


def fold_cost(nblocks):
    return pl.CostEstimate(
        flops=2 * Q * nblocks * BLK**3, bytes_accessed=nblocks << 22, transcendentals=0
    )


def fold_kernel(basis_ref, query_ref, eigen_ref, *refs):
    for q, values in folded(basis_ref, query_ref, eigen_ref):
        refs[-1][q] = values


def fold(first, last, basis_out, query, eigenvalues, partial=None):
    extra = [] if partial is None else [partial]
    return pl.pallas_call(
        fold_kernel,
        out_shape=jax.ShapeDtypeStruct(query.shape, BF16),
        grid=(last - first,),
        in_specs=fold_specs(first) + [pl.BlockSpec(memory_space=pltpu.HBM)] * len(extra),
        out_specs=pl.BlockSpec((Q, BLK, BLK), lambda b: (0, first + b, 0)),
        input_output_aliases={3: 0} if extra else {},
        cost_estimate=fold_cost(last - first),
    )(distant(basis_out), distant(query), distant(eigenvalues), *[distant(v) for v in extra])


TILE = 256
WHOLE = pl.BlockSpec(memory_space=pltpu.VMEM)
SCALARS = pl.BlockSpec(memory_space=pltpu.SMEM)
distant = lambda v: pltpu.with_memory_space_constraint(v, pltpu.HBM)
resident = lambda v: pltpu.with_memory_space_constraint(v, pltpu.VMEM)


def product_kernel(count, *refs):
    row_refs, weight_ref, far_refs = refs[:count], refs[count], refs[count + 1:]
    moved = (len(far_refs) - 1) // 2
    if moved:
        far_refs, out_ref, near_refs, sems = far_refs[:moved], far_refs[moved], far_refs[moved + 1:-1], far_refs[-1]
        copies = [
            pltpu.make_async_copy(far, near, sems.at[i]) for i, (far, near) in enumerate(zip(far_refs, near_refs))
        ]
    else:
        out_ref, copies = far_refs[0], []
    for copy in copies:
        copy.start()
    for q in range(Q):
        for part in range(BLK // TILE):
            columns = slice(part * TILE, (part + 1) * TILE)
            rows = jnp.concatenate([ref[...] for ref in row_refs], axis=0)
            out_ref[q, :, columns] = jnp.dot(rows, weight_ref[q, :, columns], preferred_element_type=F32)
    for copy in copies:
        copy.wait()


def product(rows, weight, far=()):
    height = sum(r.shape[0] for r in rows)
    depth = weight.shape[1]
    outs = pl.pallas_call(
        functools.partial(product_kernel, len(rows)),
        out_shape=(pltpu.VMEM((Q, height, BLK), F32),) + tuple(pltpu.VMEM(v.shape, v.dtype) for v in far),
        in_specs=[WHOLE] * (len(rows) + 1) + [pl.BlockSpec(memory_space=pltpu.HBM)] * len(far),
        out_specs=(WHOLE,) * (1 + len(far)),
        scratch_shapes=[pltpu.SemaphoreType.DMA((len(far),))] if far else [],
        cost_estimate=pl.CostEstimate(
            flops=2 * height * depth * Q * BLK, bytes_accessed=0, transcendentals=0
        ),
        compiler_params=pltpu.CompilerParams(vmem_limit_bytes=8 << 20),
    )(*[resident(r) for r in rows], resident(weight), *[distant(v) for v in far])
    return outs if far else outs[0]


def place(inputs, pieces, y, first):
    quarter = ROWS // 4
    for k in range(inputs.shape[0] // ROWS):
        for shift, piece in enumerate(pieces):
            start = pl.multiple_of(k * ROWS + ((y + shift) % 4) * quarter, quarter)
            inputs[pl.ds(start, quarter), :] = piece[first + k]


def narrowed(values):
    return sum([values[:, i:i + 128] for i in range(128, values.shape[1], 128)], values[:, :128])


def doc_sums(dp, offsets, ids_ref, tokens):
    docs = lax.broadcasted_iota(jnp.int32, (DOCS, ROWS), 0)
    member = jnp.concatenate(
        [(docs == ids_ref[source(dp, offset)]).astype(F32) for offset in offsets], axis=1
    ).astype(BF16)
    total = jnp.zeros((DOCS, Q * 128), F32)
    for _ in range(3):
        term = tokens.astype(BF16)
        total = total + jnp.dot(member, term, preferred_element_type=F32)
        tokens = tokens - term.astype(F32)
    return total


STRIP = 64


def settle_kernel(offsets, first, pos_ref, r0, r1, r2, r3, ids_ref, *refs):
    projected, (out_ref, inputs, tokens) = refs[:-3], refs[-3:]
    dp, y = pos_ref[0], pos_ref[1]
    place(inputs, (r0, r1, r2, r3), y, first)
    base = 0
    for ref in projected:

        def body(i, carry, ref=ref, base=base):
            here = pl.multiple_of(i * STRIP, STRIP)
            there = pl.ds(pl.multiple_of(base + here, STRIP), STRIP)
            wide = inputs[there, :].astype(F32)
            for q in range(Q):
                values = ref[q, pl.ds(here, STRIP), :] * wide
                tokens[there, q * 128:(q + 1) * 128] = narrowed(values)
            return carry

        lax.fori_loop(0, ref.shape[1] // STRIP, body, 0)
        base += ref.shape[1]
    out_ref[...] = doc_sums(dp, offsets, ids_ref, tokens[...])


def settle(position, projected, offsets, first, pieces, ids):
    height = len(offsets) * ROWS
    return pl.pallas_call(
        functools.partial(settle_kernel, offsets, first),
        out_shape=jax.ShapeDtypeStruct((DOCS, Q * 128), F32),
        in_specs=[SCALARS] + [WHOLE] * (5 + len(projected)),
        out_specs=WHOLE,
        scratch_shapes=[pltpu.VMEM((height, BLK), BF16), pltpu.VMEM((height, Q * 128), F32)],
        cost_estimate=pl.CostEstimate(
            flops=2 * height * Q * BLK, bytes_accessed=8 << 20, transcendentals=0
        ),
        compiler_params=pltpu.CompilerParams(vmem_limit_bytes=12 << 20),
    )(position, *[resident(p) for p in pieces], resident(ids), *[resident(p) for p in projected])


def score_kernel(offsets, first, pos_ref, *refs):
    row_refs, refs = refs[:-11], refs[-11:]
    weight_ref, r0, r1, r2, r3, ids_ref, before_ref, done_ref, out_ref, inputs, tokens = refs
    dp, y = pos_ref[0], pos_ref[1]
    place(inputs, (r0, r1, r2, r3), y, first)
    done = done_ref.shape[1]
    for q in range(Q):
        for part in range(BLK // TILE):
            columns = slice(part * TILE, (part + 1) * TILE)
            rows = jnp.concatenate([ref[...] for ref in row_refs], axis=0)
            values = jnp.dot(rows, weight_ref[q, :, columns], preferred_element_type=F32)
            narrow = narrowed(values * inputs[done:, columns].astype(F32))
            lanes = slice(q * 128, (q + 1) * 128)
            if part == 0:
                tokens[done:, lanes] = narrow
            else:
                tokens[done:, lanes] += narrow
    for q in range(Q):
        tokens[:done, q * 128:(q + 1) * 128] = narrowed(done_ref[q] * inputs[:done, :].astype(F32))
    sums = before_ref[...] + doc_sums(dp, offsets, ids_ref, tokens[...])
    flat = lax.dot_general(
        jnp.ones((8, 128), F32),
        jnp.concatenate([sums[:, q * 128:(q + 1) * 128] for q in range(Q)], axis=0),
        (((1,), (1,)), ((), ())),
        precision=HIGHEST,
        preferred_element_type=F32,
    )
    out_ref[...] = jnp.broadcast_to(flat[None, :1], out_ref.shape)


def score(position, rows, offsets, first, weight, pieces, ids, before, done):
    height = len(offsets) * ROWS
    depth = weight.shape[1]
    return pl.pallas_call(
        functools.partial(score_kernel, offsets, first),
        out_shape=jax.ShapeDtypeStruct((128, 1, Q * DOCS), F32),
        in_specs=[SCALARS] + [WHOLE] * (len(rows) + 8),
        out_specs=WHOLE,
        scratch_shapes=[pltpu.VMEM((height, BLK), BF16), pltpu.VMEM((height, Q * 128), F32)],
        cost_estimate=pl.CostEstimate(
            flops=2 * height * depth * Q * BLK, bytes_accessed=0, transcendentals=0
        ),
        compiler_params=pltpu.CompilerParams(vmem_limit_bytes=8 << 20),
    )(
        position,
        *[resident(r) for r in rows],
        resident(weight),
        *[resident(p) for p in pieces],
        resident(ids),
        resident(before),
        resident(done),
    )


def finish_kernel(parts_ref, out_ref):
    total = jnp.sum(parts_ref[...], axis=0) * (1.0 / math.sqrt(FF * D))
    for q in range(Q):
        out_ref[q:q + 1, :] = total[:, q * DOCS:(q + 1) * DOCS]


def move(v, perm, axis="dp"):
    return lax.ppermute(v, axis, perm)


def on_device(activations, out_grads, basis_in, basis_out, query_grads, eigenvalues, doc_ids):
    dp = lax.axis_index("dp")
    y = lax.axis_index("group") % 4
    position = jnp.stack([dp, y]).astype(jnp.int32)
    ids = doc_ids.reshape(16, 1, ROWS)

    a3 = move(out_grads, RIGHT)
    b0 = move(out_grads, ACROSS)
    a1 = move(out_grads, LEFT)
    mate = move(out_grads, MATE)

    columns = lax.all_to_all(cut(activations, position[1:]), "dp", 0, 0, tiled=True)
    turned = turn(position[:1], columns, basis_in)
    pieces = [turned] + [move(turned, y_perm(-k), "group") for k in (1, 3, 2)]
    pieces = [pieces[0], pieces[1], pieces[3], pieces[2]]

    query = jnp.transpose(query_grads, (1, 0, 2))
    weight = fold(0, basis_out.shape[0], basis_out, query, eigenvalues)

    a2 = move(a3, RIGHT)
    b3 = move(a3, ACROSS)
    b1 = move(b0, LEFT)
    step1 = [move(v, MATE) for v in (a3, a1, b0)]
    parts = [move(b3[:64], RIGHT), move(b1[64:], LEFT)]
    step2 = [move(v, MATE) for v in (a2, b1, b3)]
    step3 = [move(v, MATE) for v in parts]

    second, *near = product(step1, weight, (a3, a1, b0))
    projected = [
        product([out_grads, mate] + near, weight),
        second,
        product([a2, b1, b3], weight),
        product(step2, weight),
    ]
    total = settle(position, projected, ORDER[:14], 0, pieces, ids)
    done = product(parts, weight)
    partial = score(position, step3, ORDER[14:], 14, weight, pieces, ids, total, done)

    partials = lax.all_to_all(partial, ("dp", "group"), 0, 0, tiled=True)
    return pl.pallas_call(
        finish_kernel,
        out_shape=jax.ShapeDtypeStruct((Q, DOCS), F32),
        in_specs=[WHOLE],
        out_specs=WHOLE,
        compiler_params=pltpu.CompilerParams(vmem_limit_bytes=4 << 20),
        name="finish",
    )(resident(partials))


def solution(mesh):
    return jax.shard_map(
        on_device,
        mesh=mesh,
        in_specs=(
            P("dp", None),
            P("dp", "group"),
            P("dp", None, None),
            P("group", None, None),
            P("group", None, "dp"),
            P("group", "dp"),
            P(),
        ),
        out_specs=P(),
        check_vma=False,
    )
```
